32 devices in a mesh: row: 8 (over y, x, core), col: 4 (over z).
Axes of the slice: x: 2, y: 2, z: 4, core: 2. Of those that a mesh axis runs over, the one named last changes fastest.
Arguments:
- states: bfloat16 [128, 2, 8, 5376], P(None, None, None, 'row'), may hold values from -6 to 6
- subject_pos: int32 [128, 2], replicated, may hold values from 0 to 7
- gate_weight: bfloat16 [5376, 4, 5376], P('row', 'col'), may hold values from -0.078125 to 0.078125
- up_weight: bfloat16 [5376, 4, 5376], P('row', 'col'), may hold values from -0.078125 to 0.078125
- down_weight: bfloat16 [8, 4, 672, 5376], P('row', 'col'), may hold values from -0.0390625 to 0.0390625
- covariance: float32 [21504, 4, 5376], P('row', 'col'), as said below
- targets: float32 [5376, 128], P(('row', 'col')), may hold values from -24 to 24
Outputs:
- update: bfloat16 [8, 4, 672, 5376], P('row', 'col')
The draws below stay inside these ranges and needn't reach their ends.
Inputs may be any that keep to these rules, and one draw needn't show every extreme that they name: `covariance`: read as an 21504 x 21504 matrix (entry (i, b, a * 672 + j) in column a * 4 * 672 + b * 672 + j), it is symmetric and positive definite.
All inputs are finite; a program needn't handle non-finite values.
Results may differ from the reference program's by a relative error of at most 0.0016.
Values sent between devices are 32-bit elements; how exact they have to be, the bound alone decides.
No kernel may reach another device: no remote copies, remote signals or barrier semaphores. Data moves between devices by JAX's collectives and lax.ppermute only.
A program may use at most 192 MiB of HBM per device.

```python
import math
import jax
import jax.numpy as jnp
from jax import lax

D = 5376
FF = 21504
EDITS = 128
PREF = 2
SEQ = 8
ITERS = 2
PIECE = 672
N_ROW = 8
N_COL = 4


def draw_covariance(key, part):
    first = jax.random.fold_in(key, 11)
    second = jax.random.fold_in(key, 23)
    noise = jax.random.normal(first, (FF, FF), jnp.float32)
    diagonal = jnp.exp(jax.random.uniform(second, (FF,), jnp.float32, math.log(1.2), math.log(4.0)))
    spread = 0.4 / math.sqrt(2.0 * FF)
    matrix = (noise + noise.T) * spread
    places = jnp.arange(FF)
    matrix = matrix.at[places, places].add(diagonal)
    stored = matrix.reshape(FF, N_ROW, N_COL, PIECE).transpose(0, 2, 1, 3)
    return stored.reshape(FF, N_COL, N_ROW * PIECE)


def with_ends(entries, rng, least, high):
    longest = entries.shape.index(max(entries.shape))
    spots = []
    for shift in (0, 1):
        where = [jax.random.randint(jax.random.fold_in(rng, axis), (), 0, length) for axis, length in enumerate(entries.shape)]
        where[longest] = (where[longest] + shift) % entries.shape[longest]
        spots.append(tuple(where))
    return entries.at[spots[0]].set(least).at[spots[1]].set(high)


def block_levels(key, extent, pieces, low, high):
    level, own = 1.0, jax.random.fold_in(key, 6)
    for dim, parts in pieces:
        draws = jnp.exp(jax.random.uniform(jax.random.fold_in(own, dim), (parts,), jnp.float32, low / len(pieces), high / len(pieces)))
        level = level * jnp.repeat(draws, extent[dim] // parts).reshape([-1 if axis == dim else 1 for axis in range(len(extent))])
    return level


def centred(key, shape, deviation, most, shards=(), dtype=jnp.bfloat16):
    result = deviation * jax.random.normal(key, shape, jnp.float32)
    if shards:
        result = result * block_levels(key, shape, shards, -0.22, 0.18)
    return jnp.clip(result, -most, most).astype(dtype)


def setup_inputs(seed: int = 0) -> dict:
    seeds = jax.random.split(jax.random.key(seed), 8)
    return {
        "states": centred(seeds[0], (EDITS, PREF, SEQ, D), 1.0, 6.0, ((3, 8),)),
        "subject_pos": with_ends(jax.random.randint(seeds[1], (EDITS, PREF), 0, SEQ), jax.random.fold_in(seeds[1], 1), 0, SEQ - 1).astype(jnp.int32),
        "gate_weight": centred(seeds[2], (D, N_COL, N_ROW * PIECE), D ** -0.5, 0.078125, ((0, 8), (1, 4))),
        "up_weight": centred(seeds[3], (D, N_COL, N_ROW * PIECE), D ** -0.5, 0.078125, ((0, 8), (1, 4))),
        "down_weight": centred(seeds[4], (N_ROW, N_COL, PIECE, D), FF ** -0.5, 0.0390625, ((0, 8), (1, 4))),
        "covariance": draw_covariance(jax.random.fold_in(seeds[7], 71), 0),
        "targets": centred(seeds[6], (D, EDITS), 4.0, 24.0, ((0, 32),), jnp.float32),
    }


def high_dot(left, right):
    return jnp.dot(left.astype(jnp.float32), right.astype(jnp.float32), precision=lax.Precision.HIGHEST, preferred_element_type=jnp.float32)

def small_solve(matrix, right):
    factor = jnp.linalg.cholesky(matrix)
    return jax.scipy.linalg.cho_solve((factor, True), right)

def symmetric(matrix):
    return 0.5 * (matrix + matrix.T)

def hidden_order(stored, leading):
    return stored.reshape(leading, N_COL, N_ROW, PIECE).transpose(0, 2, 1, 3).reshape(leading, FF)

def reference(states, subject_pos, gate_weight, up_weight, down_weight, covariance, targets):
    index = subject_pos.astype(jnp.int32)[:, :, None, None]
    chosen = jnp.take_along_axis(states, index, axis=2)[:, :, 0, :]
    token_rows = chosen.reshape(EDITS * PREF, D)
    gate = jnp.dot(token_rows.astype(jnp.float32), hidden_order(gate_weight, D).astype(jnp.float32), preferred_element_type=jnp.float32)
    up_value = jnp.dot(token_rows.astype(jnp.float32), hidden_order(up_weight, D).astype(jnp.float32), preferred_element_type=jnp.float32)
    hidden = jax.nn.silu(gate) * up_value
    keys = lax.optimization_barrier(jnp.mean(hidden.reshape(EDITS, PREF, FF), axis=1)).T
    keys_half = keys.astype(jnp.bfloat16)
    current = jnp.dot(down_weight.reshape(FF, D).T.astype(jnp.float32), keys_half.astype(jnp.float32), preferred_element_type=jnp.float32)
    residual_t = targets - current
    matrix = hidden_order(covariance, FF)
    basis = 4.0 / math.sqrt(FF) * keys
    solution = jnp.zeros_like(basis)
    resid = basis
    direction = basis
    norm_now = symmetric(high_dot(resid.T, resid))
    for step in range(ITERS):
        image = high_dot(matrix, direction) + high_dot(basis, high_dot(basis.T, direction))
        curvature = symmetric(high_dot(direction.T, image))
        alpha = small_solve(curvature, norm_now)
        solution = solution + high_dot(direction, alpha)
        resid = resid - high_dot(image, alpha)
        if step + 1 < ITERS:
            norm_next = symmetric(high_dot(resid.T, resid))
            beta = small_solve(norm_now, norm_next)
            direction = resid + high_dot(direction, beta)
            norm_now = norm_next
    update = high_dot(solution, residual_t.T)
    return update.reshape(N_ROW, N_COL, PIECE, D).astype(jnp.bfloat16)
```

```python
import functools
import math

import jax
import jax.numpy as jnp
from jax import lax
from jax.experimental import pallas as pl
from jax.experimental.pallas import tpu as pltpu
from jax.sharding import PartitionSpec as P

HIGHEST = lax.Precision.HIGHEST
F32 = jnp.float32
BF16 = jnp.bfloat16


def dot(left, right, contract=((1,), (0,)), precision=HIGHEST):
    return lax.dot_general(left, right, (contract, ((), ())), precision=precision, preferred_element_type=F32)


def symmetric(matrix):
    return 0.5 * (matrix + matrix.T)


def solve_kernel(*refs, systems):
    mats, rights, outs, (held, panel) = refs[:systems], refs[systems : 2 * systems], refs[2 * systems : -2], refs[-2:]
    size = mats[0].shape[0]
    lanes = lax.broadcasted_iota(jnp.int32, (8, size), 1)
    subs = lax.broadcasted_iota(jnp.int32, (8, 2 * size), 0)
    all_lanes = lax.broadcasted_iota(jnp.int32, (size, size), 1)
    all_rows = lax.broadcasted_iota(jnp.int32, (size, 2 * size), 0)
    for q in range(systems):
        held[q, :, :size] = mats[q][...]
        held[q, :, size:] = rights[q][...]
    panel[...] = jnp.zeros_like(panel)

    def step(block, carry):
        base = pl.multiple_of(block * 8, 8)
        for q in range(systems):
            rows = held[q, pl.ds(base, 8), :]
            left = rows[:, :size]
            cols = [
                jnp.broadcast_to(jnp.sum(jnp.where(lanes == base + j, left, 0.0), axis=1, keepdims=True), (8, size))
                for j in range(8)
            ]
            for k in range(8):
                inverse = 1.0 / cols[k][k : k + 1, :]
                wide = jnp.concatenate([inverse, inverse], axis=1)
                factor = jnp.concatenate([cols[k], cols[k]], axis=1)
                pivot = rows[k : k + 1, :] * wide
                rows = jnp.where(subs == k, pivot, rows - factor * pivot)
                for j in range(k + 1, 8):
                    scaled = cols[j][k : k + 1, :] * inverse
                    cols[j] = jnp.where(subs[:, :size] == k, scaled, cols[j] - cols[k] * scaled)
            panel[q, pl.ds(base, 8), :] = rows
            whole = held[q]
            inside = (all_lanes >= base) & (all_lanes < base + 8)
            change = dot(jnp.where(inside, whole[:, :size], 0.0), panel[q])
            within = (all_rows >= base) & (all_rows < base + 8)
            held[q] = jnp.where(within, panel[q], whole - change)
            panel[q, pl.ds(base, 8), :] = jnp.zeros((8, 2 * size), F32)
        return carry

    lax.fori_loop(0, size // 8, step, 0)
    for q in range(systems):
        outs[q][...] = held[q, :, size:]


def solve(*pairs):
    count, size = len(pairs), pairs[0][0].shape[0]
    spec = pl.BlockSpec(memory_space=pltpu.VMEM)
    return pl.pallas_call(
        functools.partial(solve_kernel, systems=count),
        out_shape=(jax.ShapeDtypeStruct((size, size), F32),) * count,
        in_specs=[spec] * (2 * count),
        out_specs=(spec,) * count,
        scratch_shapes=[pltpu.VMEM((count, size, 2 * size), F32)] * 2,
        name="solve",
    )(*[m for m, _ in pairs], *[r for _, r in pairs])


def trade(x, axis, bit, n):
    return lax.ppermute(x, axis, [(i, i ^ bit) for i in range(n)])


def fetch(x, axis, k, n):
    return lax.ppermute(x, axis, [((i + k) % n, i) for i in range(n)])


def bit_orders(n):
    upper = [1 << b for b in range(1, n.bit_length() - 1)]
    return upper, upper[::-1]


def sum_all(x, row, col):
    x = x + trade(x, "row", 1, row)
    x = sum([trade(x, "row", k, row) for k in range(2, row, 2)], x)
    return sum_col(x, col)


def sum_col(x, col):
    return sum([fetch(x, "col", k, col) for k in range(1, col)], x)


def reduce_rows(chunks, n):
    crossed = [trade(send, "row", 1, n) for _, send in chunks]
    held = []
    for (keep, _), got in zip(chunks, crossed):
        width = keep.shape[2] // 2
        both = keep + got
        for color in range(2):
            held.append({s: both[s // 2, :, color * width : (color + 1) * width] for s in range(0, n, 2)})
    orders = bit_orders(n)
    for level in range(len(orders[0])):
        moved = []
        for at, parts in enumerate(held):
            bit = orders[at % 2][level]
            going = [s for s in parts if s & bit]
            moved.append((bit, going, trade(jnp.stack([parts[s] for s in going]), "row", bit, n)))
        for parts, (bit, going, got) in zip(held, moved):
            for place, s in enumerate(going):
                parts[s ^ bit] = parts[s ^ bit] + got[place]
                del parts[s]
    return [jnp.concatenate([held[2 * k][0], held[2 * k + 1][0]], axis=1) for k in range(len(chunks))]


def halves(p):
    first = (p // 2 + 7) // 8 * 8
    return (0, first), (first, p)


def gather_rows(own, n):
    parts = []
    for (start, stop), order in zip(halves(own.shape[0]), bit_orders(n)):
        stack, slots = own[None, start:stop], [0]
        for bit in order:
            stack = jnp.concatenate([stack, trade(stack, "row", bit, n)])
            slots = slots + [s ^ bit for s in slots]
        parts.append((start, stack, slots))
        parts.append((start, trade(stack, "row", 1, n), [s ^ 1 for s in slots]))
    return parts


def gather_cols(own, n):
    return [own] + [fetch(own, "col", k, n) for k in range(1, n)]


def reduce_cols(slots, n):
    if n != 4:
        return sum([fetch(slots[n - k], "col", k, n) for k in range(1, n)], slots[0])
    (a, b), (_, c) = halves(slots[0].shape[0])
    low = fetch(slots[2][a:b], "col", n - 1, n)
    high = fetch(slots[2][b:c], "col", 1, n)
    right = jnp.concatenate([slots[1][a:b] + low, slots[1][b:c]])
    left = jnp.concatenate([slots[3][a:b], slots[3][b:c] + high])
    return slots[0] + fetch(right, "col", n - 1, n) + fetch(left, "col", 1, n)


def project_kernel(place, x_ref, weight_ref, keep_ref, send_ref, acc, sems, *, n, piece, tile):
    step = pl.program_id(0)
    rows = pl.ds(pl.multiple_of(step * tile, 128), tile)
    acc[rows, :] = dot(weight_ref[...], x_ref[...], ((0,), (1,)), None)
    for a in range(n):
        slot = jnp.bitwise_xor(place[0], a)
        source = acc.at[pl.ds(a * piece, piece)]

        @pl.when(step == (a * piece + piece - 1) // tile)
        def _():
            @pl.when(slot % 2 == 0)
            def _():
                pltpu.make_async_copy(source, keep_ref.at[slot // 2], sems.at[a]).start()

            @pl.when(slot % 2 == 1)
            def _():
                pltpu.make_async_copy(source, send_ref.at[slot // 2], sems.at[a]).start()

    @pl.when(step == pl.num_programs(0) - 1)
    def _():
        for a in range(n):
            pltpu.make_async_copy(acc.at[pl.ds(a * piece, piece)], keep_ref.at[0], sems.at[a]).wait()


def project(place, x, weight, n, piece):
    depth, columns = weight.shape
    tokens = x.shape[0]
    tile = columns // 7
    shape = jax.ShapeDtypeStruct((n // 2, piece, tokens), F32)
    return pl.pallas_call(
        functools.partial(project_kernel, n=n, piece=piece, tile=tile),
        out_shape=(shape, shape),
        grid_spec=pltpu.PrefetchScalarGridSpec(
            num_scalar_prefetch=1,
            grid=(columns // tile,),
            in_specs=[
                pl.BlockSpec((tokens, depth), lambda i, s: (0, 0)),
                pl.BlockSpec((depth, tile), lambda i, s: (0, i)),
            ],
            out_specs=[pl.BlockSpec(memory_space=pl.ANY)] * 2,
            scratch_shapes=[pltpu.VMEM((columns, tokens), F32), pltpu.SemaphoreType.DMA((n,))],
        ),
        compiler_params=pltpu.CompilerParams(dimension_semantics=("arbitrary",), vmem_limit_bytes=50 << 20),
        cost_estimate=pl.CostEstimate(
            flops=2 * depth * columns * tokens,
            transcendentals=0,
            bytes_accessed=2 * depth * columns + 4 * columns * tokens,
        ),
        name="project",
    )(place, x, weight)


def split(value):
    high = value.astype(BF16)
    return high, (value - high.astype(F32)).astype(BF16)


def place_parts(place, parts, refs, target, piece):
    for (start, size, slots), ref in zip(parts, refs):
        for k, s in enumerate(slots):
            at = jnp.bitwise_xor(place[0], s) * piece + start
            target[pl.ds(pl.multiple_of(at, 8), size), :] = ref[k]


def describe(parts):
    return tuple((start, stack.shape[1], tuple(slots)) for start, stack, slots in parts)


VM = pl.BlockSpec(memory_space=pltpu.VMEM)
SM = pl.BlockSpec(memory_space=pltpu.SMEM)


def triple(left, pair, contract=((1,), (0,))):
    high, low = split(left)
    edits = pair.shape[1] // 2
    main = dot(high, pair, contract, None)
    return main[:, :edits] + (main[:, edits:] + dot(low, pair[:, :edits], contract, None))


def residual_kernel(place, wide_b, alpha, *refs, parts, piece, cols):
    ins, talls, images = refs[: len(parts)], refs[len(parts) :][:cols], refs[len(parts) + cols :][:cols]
    tall, pair, grams, image = refs[-4:]
    place_parts(place, parts, ins, image, piece)
    factor = alpha[...]
    value = wide_b[...] - dot(image[...], factor)
    for k in range(cols):
        tall[k * piece : (k + 1) * piece, :] = talls[k][...] - dot(images[k][...], factor)
    edits = factor.shape[0]
    high, low = split(value)
    pair[:, :edits] = high
    pair[:, edits:] = low
    across = ((0,), (0,))
    both = pair[...]
    grams[:edits] = triple(value, both, across)
    grams[edits : 2 * edits] = triple(wide_b[...], both, across)
    grams[2 * edits :] = triple(image[...], both, across)


def residual_step(place, wide_b, alpha, parts, talls, images, piece, row):
    edits = alpha.shape[0]
    col = len(talls)
    ins = [stack for _, stack, _ in parts] + talls + images
    return pl.pallas_call(
        functools.partial(residual_kernel, parts=describe(parts), piece=piece, cols=col),
        out_shape=(
            jax.ShapeDtypeStruct((col * piece, edits), F32),
            jax.ShapeDtypeStruct((row * piece, 2 * edits), BF16),
            jax.ShapeDtypeStruct((3 * edits, edits), F32),
        ),
        in_specs=[SM] + [VM] * (2 + len(ins)),
        out_specs=(VM,) * 3,
        scratch_shapes=[pltpu.VMEM((row * piece, edits), F32)],
        compiler_params=pltpu.CompilerParams(vmem_limit_bytes=56 << 20),
        name="residual_step",
    )(place, wide_b, alpha, *ins)


def apply_block(cov_ref, pair_ref, high, low, tile, chunks):
    for k in range(chunks):
        high[:, k * 128 : (k + 1) * 128], low[:, k * 128 : (k + 1) * 128] = split(
            cov_ref[pl.ds(k, tile, stride=chunks), :]
        )
    edits = pair_ref.shape[1] // 2
    main = dot(high[...], pair_ref[...], precision=None)
    return main[:, :edits] + (main[:, edits:] + dot(low[...], pair_ref[:, :edits], precision=None))


def first_kernel(place, cov_ref, *refs, parts, piece, tile, chunks):
    ins, (out, wide, pair, high, low) = refs[: len(parts)], refs[len(parts) :]

    @pl.when(pl.program_id(0) == 0)
    def _():
        place_parts(place, parts, ins, wide, piece)
        edits = wide.shape[1]
        pair[:, :edits], pair[:, edits:] = split(wide[...])

    out[...] = apply_block(cov_ref, pair, high, low, tile, chunks)


def second_kernel(place, cov_ref, pair_ref, side, gram, high, low, *, tile, chunks):
    value = apply_block(cov_ref, pair_ref, high, low, tile, chunks)

    @pl.when(pl.program_id(0) == 0)
    def _():
        gram[...] = jnp.zeros_like(gram)

    gram[...] += dot(side[...], value, ((0,), (0,)))


def tiling(piece, col):
    tile = piece
    while tile > 336 and tile % 16 == 0:
        tile //= 2
    per = piece // tile
    slot = lambda i, s: (lax.rem(i // per + col - s[1], col) * per + i % per, 0)
    return tile, slot


def operate(kernel, place, cov, shapes, ins, specs, outs, scratch, tile, edits):
    rows, _, columns = cov.shape
    chunks = columns // 128
    return pl.pallas_call(
        functools.partial(kernel, tile=tile, chunks=chunks),
        out_shape=shapes,
        grid_spec=pltpu.PrefetchScalarGridSpec(
            num_scalar_prefetch=1,
            grid=(rows // tile,),
            in_specs=[pl.BlockSpec((tile * chunks, 128), lambda i, s: (i, 0))] + specs,
            out_specs=outs,
            scratch_shapes=scratch + [pltpu.VMEM((tile, columns), BF16)] * 2,
        ),
        compiler_params=pltpu.CompilerParams(dimension_semantics=("arbitrary",), vmem_limit_bytes=60 << 20),
        cost_estimate=pl.CostEstimate(
            flops=6 * rows * columns * edits, transcendentals=0, bytes_accessed=4 * rows * columns
        ),
        name=kernel.func.__name__ if isinstance(kernel, functools.partial) else kernel.__name__,
    )(place, cov.reshape(rows * chunks, 128), *ins)


def operate_first(place, cov, parts, piece, col):
    rows, _, columns = cov.shape
    edits = parts[0][1].shape[2]
    tile, slot = tiling(piece, col)
    ins = [stack for _, stack, _ in parts]
    return operate(
        functools.partial(first_kernel, parts=describe(parts), piece=piece),
        place,
        cov,
        (jax.ShapeDtypeStruct((rows, edits), F32), jax.ShapeDtypeStruct((columns, edits), F32)),
        ins,
        [pl.BlockSpec(stack.shape, lambda i, s: (0, 0, 0)) for stack in ins],
        (pl.BlockSpec((tile, edits), slot), pl.BlockSpec((columns, edits), lambda i, s: (0, 0))),
        [pltpu.VMEM((columns, 2 * edits), BF16)],
        tile,
        edits,
    )


def operate_second(place, cov, pair, side, piece, col):
    columns, edits = pair.shape[0], pair.shape[1] // 2
    tile, slot = tiling(piece, col)
    return operate(
        second_kernel,
        place,
        cov,
        jax.ShapeDtypeStruct((edits, edits), F32),
        [pair, side],
        [pl.BlockSpec((columns, 2 * edits), lambda i, s: (0, 0)), pl.BlockSpec((tile, edits), slot)],
        pl.BlockSpec((edits, edits), lambda i, s: (0, 0)),
        [],
        tile,
        edits,
    )


def update_kernel(basis, direct, alphas, resid_ref, out_ref, held):
    @pl.when(pl.program_id(0) == 0)
    def _():
        value = dot(basis[...], alphas[0]) + dot(direct[...], alphas[1])
        high, low = split(value)
        held[:, :128] = high
        held[:, 128:] = low

    high, low = split(resid_ref[...])
    across = ((1,), (1,))
    edits = high.shape[1]
    value = dot(held[:, :edits], high, across, None) + (
        dot(held[:, edits:], high, across, None) + dot(held[:, :edits], low, across, None)
    )
    out_ref[...] = value.astype(out_ref.dtype)


def update_step(basis, direct, alphas, resid):
    rows, edits = basis.shape
    features = resid.shape[0]
    tile = features // 7
    whole = pl.BlockSpec((rows, edits), lambda i: (0, 0))
    return pl.pallas_call(
        update_kernel,
        out_shape=jax.ShapeDtypeStruct((rows, features), BF16),
        grid=(7,),
        in_specs=[
            whole,
            whole,
            pl.BlockSpec((2, edits, edits), lambda i: (0, 0, 0)),
            pl.BlockSpec((tile, edits), lambda i: (i, 0)),
        ],
        out_specs=pl.BlockSpec((rows, tile), lambda i: (0, i)),
        scratch_shapes=[pltpu.VMEM((rows, 2 * edits), BF16)],
        compiler_params=pltpu.CompilerParams(dimension_semantics=("arbitrary",)),
        name="update_step",
    )(basis, direct, alphas, resid)


def body(states, subject_pos, gate_weight, up_weight, down_weight, covariance, targets, *, row, col):
    edits, prompts, seq_len, _ = states.shape
    piece = down_weight.shape[2]
    hidden_units = row * col * piece
    place = jnp.stack([lax.axis_index("row"), lax.axis_index("col")]).astype(jnp.int32)
    marks = lax.broadcasted_iota(jnp.int32, (1, 1, seq_len, 1), 2) == subject_pos[:, :, None, None]
    chosen = jnp.sum(jnp.where(marks, states, jnp.zeros_like(states)), axis=2)
    token_rows = chosen.transpose(1, 0, 2).reshape(prompts * edits, -1)

    flat = [w.reshape(w.shape[0], -1) for w in (gate_weight, up_weight)]
    gate, up = reduce_rows([project(place, token_rows, w, row, piece) for w in flat], row)
    hidden = jax.nn.silu(gate) * up
    keys = sum(hidden[:, p * edits : (p + 1) * edits] for p in range(prompts)) / prompts
    basis = 4.0 / math.sqrt(hidden_units) * keys
    across = ((0,), (0,))

    wide_parts = gather_rows(basis, row)
    talls = gather_cols(basis, col)
    norm = symmetric(sum_all(dot(basis, basis, across), row, col))
    current = lax.psum_scatter(
        dot(down_weight.reshape(piece, -1), keys.astype(BF16), across, None),
        ("row", "col"),
        scatter_dimension=0,
        tiled=True,
    )

    partial, wide_b = operate_first(place, covariance, wide_parts, piece, col)
    slots = [partial[k * piece : (k + 1) * piece] for k in range(col)]
    inner = sum(dot(tall, slot, across) for tall, slot in zip(talls, slots))
    image = reduce_cols(slots, col) + dot(basis, norm)
    first = sum_all(inner, row, col) + dot(norm, norm)
    alpha, norm_inverse = solve((symmetric(first), norm), (norm, jnp.eye(edits, dtype=F32)))

    tall_r, pair_r, grams = residual_step(
        place, wide_b, alpha, gather_rows(image, row), talls, gather_cols(image, col), piece, row
    )
    current, pair_r = lax.optimization_barrier((current, pair_r))
    residual_t = lax.all_gather(targets - current, ("row", "col"), axis=0, tiled=True)
    resid = basis - dot(image, alpha)
    grams = sum_col(grams, col)
    inner_r = operate_second(place, covariance, pair_r, tall_r, piece, col)
    norm_next = symmetric(grams[:edits])
    across_b, across_i = grams[edits : 2 * edits], grams[2 * edits :]
    beta = dot(norm_inverse, norm_next)
    direction = resid + dot(basis, beta)
    quad = sum_all(inner_r, row, col)
    mixed = across_i
    curvature = quad + dot(across_b.T, across_b) + dot(beta.T, mixed) + dot(mixed.T, beta)
    curvature = curvature + dot(beta.T, dot(first, beta))
    (alpha_last,) = solve((symmetric(curvature), norm_next))
    update = update_step(basis, direction, jnp.stack([alpha, alpha_last]), residual_t)
    return update.reshape(1, 1, piece, -1)


def solution(mesh):
    return jax.shard_map(
        functools.partial(body, row=mesh.shape["row"], col=mesh.shape["col"]),
        mesh=mesh,
        in_specs=(
            P(None, None, None, "row"),
            P(),
            P("row", "col", None),
            P("row", "col", None),
            P("row", "col", None, None),
            P("row", "col", None),
            P(("row", "col"), None),
        ),
        out_specs=P("row", "col", None, None),
        check_vma=False,
    )
```

```python
import functools
import math

import jax
import jax.numpy as jnp
from jax import lax
from jax.experimental import pallas as pl
from jax.experimental.pallas import tpu as pltpu
from jax.experimental.layout import Layout, with_layout_constraint
from jax.sharding import PartitionSpec as P

HIGHEST = lax.Precision.HIGHEST
F32 = jnp.float32
BF16 = jnp.bfloat16


def dot(left, right, contract=((1,), (0,)), precision=HIGHEST):
    return lax.dot_general(left, right, (contract, ((), ())), precision=precision, preferred_element_type=F32)


def symmetric(matrix):
    return 0.5 * (matrix + matrix.T)


def solve_kernel(*refs, systems):
    mats, rights, outs, (held, panel) = refs[:systems], refs[systems : 2 * systems], refs[2 * systems : -2], refs[-2:]
    size = mats[0].shape[0]
    lanes = lax.broadcasted_iota(jnp.int32, (8, size), 1)
    subs = lax.broadcasted_iota(jnp.int32, (8, 2 * size), 0)
    all_lanes = lax.broadcasted_iota(jnp.int32, (size, size), 1)
    all_rows = lax.broadcasted_iota(jnp.int32, (size, 2 * size), 0)
    for q in range(systems):
        held[q, :, :size] = mats[q][...]
        held[q, :, size:] = rights[q][...]
    panel[...] = jnp.zeros_like(panel)

    def step(block, carry):
        base = pl.multiple_of(block * 8, 8)
        every = range(systems)
        rows = [held[q, pl.ds(base, 8), :] for q in every]
        cols = [
            [
                jnp.broadcast_to(
                    jnp.sum(jnp.where(lanes == base + j, rows[q][:, :size], 0.0), axis=1, keepdims=True), (8, size)
                )
                for j in range(8)
            ]
            for q in every
        ]
        for k in range(8):
            inverse = [1.0 / cols[q][k][k : k + 1, :] for q in every]
            for q in every:
                pivot = rows[q][k : k + 1, :] * jnp.concatenate([inverse[q]] * 2, axis=1)
                factor = jnp.concatenate([cols[q][k]] * 2, axis=1)
                rows[q] = jnp.where(subs == k, pivot, rows[q] - factor * pivot)
                for j in range(k + 1, 8):
                    scaled = cols[q][j][k : k + 1, :] * inverse[q]
                    cols[q][j] = jnp.where(subs[:, :size] == k, scaled, cols[q][j] - cols[q][k] * scaled)
        inside = (all_lanes >= base) & (all_lanes < base + 8)
        within = (all_rows >= base) & (all_rows < base + 8)
        for q in every:
            panel[q, pl.ds(base, 8), :] = rows[q]
        whole = [held[q] for q in every]
        filled = [panel[q] for q in every]
        change = [dot(jnp.where(inside, whole[q][:, :size], 0.0), filled[q]) for q in every]
        for q in every:
            held[q] = jnp.where(within, filled[q], whole[q] - change[q])
            panel[q, pl.ds(base, 8), :] = jnp.zeros((8, 2 * size), F32)
        return carry

    lax.fori_loop(0, size // 8, step, 0)
    for q in range(systems):
        outs[q][...] = held[q, :, size:]


def solve(*pairs):
    count, size = len(pairs), pairs[0][0].shape[0]
    spec = pl.BlockSpec(memory_space=pltpu.VMEM)
    return pl.pallas_call(
        functools.partial(solve_kernel, systems=count),
        out_shape=(jax.ShapeDtypeStruct((size, size), F32),) * count,
        in_specs=[spec] * (2 * count),
        out_specs=(spec,) * count,
        scratch_shapes=[pltpu.VMEM((count, size, 2 * size), F32)] * 2,
        name="solve",
    )(*[m for m, _ in pairs], *[r for _, r in pairs])


def trade(x, axis, bit, n):
    return lax.ppermute(x, axis, [(i, i ^ bit) for i in range(n)])


def fetch(x, axis, k, n):
    return lax.ppermute(x, axis, [((i + k) % n, i) for i in range(n)])


def bit_orders(n):
    upper = [1 << b for b in range(1, n.bit_length() - 1)]
    return upper, upper[::-1]


def sum_all(x, row, col):
    x = x + trade(x, "row", 1, row)
    x = sum([trade(x, "row", k, row) for k in range(2, row, 2)], x)
    return sum_col(x, col)


def sum_col(x, col):
    return sum(fetch_all(x, col), x)


def fetch_all(x, col):
    return [fetch(x, "col", k, col) for k in range(1, col)]


def reduce_rows(chunks, n):
    crossed = []
    for _, send in chunks:
        crossed.append(trade(send, "row", 1, n))
    held = []
    for (keep, _), got in zip(chunks, crossed):
        width = keep.shape[2] // 2
        both = keep + got
        for color in range(2):
            held.append({s: both[s // 2, :, color * width : (color + 1) * width] for s in range(0, n, 2)})
    orders = bit_orders(n)
    for level in range(len(orders[0])):
        moved = []
        for at, parts in enumerate(held):
            bit = orders[at % 2][level]
            going = [s for s in parts if s & bit]
            moved.append((bit, going, trade(jnp.stack([parts[s] for s in going]), "row", bit, n)))
        for parts, (bit, going, got) in zip(held, moved):
            for place, s in enumerate(going):
                parts[s ^ bit] = parts[s ^ bit] + got[place]
                del parts[s]
    return [jnp.concatenate([held[2 * k][0], held[2 * k + 1][0]], axis=1) for k in range(len(chunks))]


def halves(p):
    first = (p // 2 + 7) // 8 * 8
    return (0, first), (first, p)


def gather_rows(own, n):
    parts = []
    for (start, stop), order in zip(halves(own.shape[0]), bit_orders(n)):
        stack, slots = own[None, start:stop], [0]
        for bit in order:
            got = trade(stack, "row", bit, n)
            stack = jnp.concatenate([stack, got])
            slots = slots + [s ^ bit for s in slots]
        parts.append((start, stack, slots))
        parts.append((start, trade(stack, "row", 1, n), [s ^ 1 for s in slots]))
    return parts


def gather_cols(own, n):
    if n != 4:
        return [own] + fetch_all(own, n)
    (a, b), (_, c) = halves(own.shape[0])
    after, before = fetch(own, "col", 1, n), fetch(own, "col", n - 1, n)
    low, high = fetch(after[a:b], "col", 1, n), fetch(before[b:c], "col", n - 1, n)
    return [own, after, jnp.concatenate([low, high]), before]


def reduce_cols(slots, n):
    if n != 4:
        return sum([fetch(slots[n - k], "col", k, n) for k in range(1, n)], slots[0])
    (a, b), (_, c) = halves(slots[0].shape[0])
    low = fetch(slots[2][a:b], "col", n - 1, n)
    high = fetch(slots[2][b:c], "col", 1, n)
    right = jnp.concatenate([slots[1][a:b] + low, slots[1][b:c]])
    left = jnp.concatenate([slots[3][a:b], slots[3][b:c] + high])
    return slots[0] + fetch(right, "col", n - 1, n) + fetch(left, "col", 1, n)


def project_kernel(place, x_ref, weight_ref, keep_ref, send_ref, acc, sems, *, n, piece, tile):
    step = pl.program_id(0)
    rows = pl.ds(pl.multiple_of(step * tile, 128), tile)
    acc[rows, :] = dot(weight_ref[...], x_ref[...], ((0,), (1,)), None)
    for a in range(n):
        slot = jnp.bitwise_xor(place[0], a)
        source = acc.at[pl.ds(a * piece, piece)]

        @pl.when(step == (a * piece + piece - 1) // tile)
        def _():
            @pl.when(slot % 2 == 0)
            def _():
                pltpu.make_async_copy(source, keep_ref.at[slot // 2], sems.at[a]).start()

            @pl.when(slot % 2 == 1)
            def _():
                pltpu.make_async_copy(source, send_ref.at[slot // 2], sems.at[a]).start()

    @pl.when(step == pl.num_programs(0) - 1)
    def _():
        for a in range(n):
            pltpu.make_async_copy(acc.at[pl.ds(a * piece, piece)], keep_ref.at[0], sems.at[a]).wait()


def project(place, x, weight, n, piece):
    depth, columns = weight.shape
    tokens = x.shape[0]
    tile = columns // 7
    shape = jax.ShapeDtypeStruct((n // 2, piece, tokens), F32)
    return pl.pallas_call(
        functools.partial(project_kernel, n=n, piece=piece, tile=tile),
        out_shape=(shape, shape),
        grid_spec=pltpu.PrefetchScalarGridSpec(
            num_scalar_prefetch=1,
            grid=(columns // tile,),
            in_specs=[
                pl.BlockSpec((tokens, depth), lambda i, s: (0, 0)),
                pl.BlockSpec((depth, tile), lambda i, s: (0, i)),
            ],
            out_specs=[pl.BlockSpec(memory_space=pl.ANY)] * 2,
            scratch_shapes=[pltpu.VMEM((columns, tokens), F32), pltpu.SemaphoreType.DMA((n,))],
        ),
        compiler_params=pltpu.CompilerParams(dimension_semantics=("arbitrary",), vmem_limit_bytes=50 << 20),
        cost_estimate=pl.CostEstimate(
            flops=2 * depth * columns * tokens,
            transcendentals=0,
            bytes_accessed=2 * depth * columns + 4 * columns * tokens,
        ),
        name="project",
    )(place, x, weight)


def split(value):
    high = value.astype(BF16)
    return high, (value - high.astype(F32)).astype(BF16)


def place_parts(place, parts, refs, target, piece):
    for (start, size, slots), ref in zip(parts, refs):
        for k, s in enumerate(slots):
            at = jnp.bitwise_xor(place[0], s) * piece + start
            target[pl.ds(pl.multiple_of(at, 8), size), :] = ref[k]


def describe(parts):
    return tuple((start, stack.shape[1], tuple(slots)) for start, stack, slots in parts)


VM = pl.BlockSpec(memory_space=pltpu.VMEM)
SM = pl.BlockSpec(memory_space=pltpu.SMEM)


def triple(left, pair, contract=((1,), (0,))):
    high, low = split(left)
    edits = pair.shape[1] // 2
    main = dot(high, pair, contract, None)
    return main[:, :edits] + (main[:, edits:] + dot(low, pair[:, :edits], contract, None))


def residual_kernel(place, wide_b, alpha, *refs, parts, piece):
    ins, (pair, grams, image) = refs[: len(parts)], refs[len(parts) :]
    place_parts(place, parts, ins, image, piece)
    factor = alpha[...]
    value = wide_b[...] - dot(image[...], factor)
    edits = factor.shape[0]
    high, low = split(value)
    pair[:, :edits] = high
    pair[:, edits:] = low
    across = ((0,), (0,))
    both = pair[...]
    grams[:edits] = triple(value, both, across)
    grams[edits:] = triple(image[...], both, across)


def residual_step(place, wide_b, alpha, parts, piece, row):
    edits = alpha.shape[0]
    ins = [stack for _, stack, _ in parts]
    return pl.pallas_call(
        functools.partial(residual_kernel, parts=describe(parts), piece=piece),
        out_shape=(
            jax.ShapeDtypeStruct((row * piece, 2 * edits), BF16),
            jax.ShapeDtypeStruct((2 * edits, edits), F32),
        ),
        in_specs=[SM] + [VM] * (2 + len(ins)),
        out_specs=(VM,) * 2,
        scratch_shapes=[pltpu.VMEM((row * piece, edits), F32)],
        compiler_params=pltpu.CompilerParams(vmem_limit_bytes=56 << 20),
        name="residual_step",
    )(place, wide_b, alpha, *ins)


def apply_block(cov_ref, pair_ref, high, low, tile, chunks):
    for k in range(chunks):
        high[:, k * 128 : (k + 1) * 128], low[:, k * 128 : (k + 1) * 128] = split(
            cov_ref[pl.ds(k, tile, stride=chunks), :]
        )
    edits = pair_ref.shape[1] // 2
    main = dot(high[...], pair_ref[...], precision=None)
    return main[:, :edits] + (main[:, edits:] + dot(low[...], pair_ref[:, :edits], precision=None))


def first_kernel(place, cov_ref, *refs, parts, piece, tile, chunks):
    ins, (out, wide, gram, pair, high, low) = refs[: len(parts)], refs[len(parts) :]

    @pl.when(pl.program_id(0) == 0)
    def _():
        place_parts(place, parts, ins, wide, piece)
        edits = wide.shape[1]
        pair[:, :edits], pair[:, edits:] = split(wide[...])
        gram[...] = triple(wide[...], pair[...], ((0,), (0,)))

    out[...] = apply_block(cov_ref, pair, high, low, tile, chunks)


def second_kernel(place, cov_ref, pair_ref, out, high, low, *, tile, chunks):
    out[...] = apply_block(cov_ref, pair_ref, high, low, tile, chunks)


def tiling(piece, col):
    tile = piece
    while tile > 336 and tile % 16 == 0:
        tile //= 2
    per = piece // tile
    slot = lambda i, s: (lax.rem(i // per + col - s[1], col) * per + i % per, 0)
    return tile, slot


def operate(kernel, place, cov, shapes, ins, specs, outs, scratch, tile, edits):
    rows, _, columns = cov.shape
    chunks = columns // 128
    return pl.pallas_call(
        functools.partial(kernel, tile=tile, chunks=chunks),
        out_shape=shapes,
        grid_spec=pltpu.PrefetchScalarGridSpec(
            num_scalar_prefetch=1,
            grid=(rows // tile,),
            in_specs=[pl.BlockSpec((tile * chunks, 128), lambda i, s: (i, 0))] + specs,
            out_specs=outs,
            scratch_shapes=scratch + [pltpu.VMEM((tile, columns), BF16)] * 2,
        ),
        compiler_params=pltpu.CompilerParams(dimension_semantics=("arbitrary",), vmem_limit_bytes=60 << 20),
        cost_estimate=pl.CostEstimate(
            flops=6 * rows * columns * edits, transcendentals=0, bytes_accessed=4 * rows * columns
        ),
    )(place, cov.reshape(rows * chunks, 128), *ins)


def operate_first(place, cov, parts, piece, col):
    rows, _, columns = cov.shape
    edits = parts[0][1].shape[2]
    tile, slot = tiling(piece, col)
    ins = [stack for _, stack, _ in parts]
    return operate(
        functools.partial(first_kernel, parts=describe(parts), piece=piece),
        place,
        cov,
        (
            jax.ShapeDtypeStruct((rows, edits), F32),
            jax.ShapeDtypeStruct((columns, edits), F32),
            jax.ShapeDtypeStruct((edits, edits), F32),
        ),
        ins,
        [pl.BlockSpec(stack.shape, lambda i, s: (0, 0, 0)) for stack in ins],
        (
            pl.BlockSpec((tile, edits), slot),
            pl.BlockSpec((columns, edits), lambda i, s: (0, 0)),
            pl.BlockSpec((edits, edits), lambda i, s: (0, 0)),
        ),
        [pltpu.VMEM((columns, 2 * edits), BF16)],
        tile,
        edits,
    )


def operate_second(place, cov, pair, piece, col):
    columns, edits = pair.shape[0], pair.shape[1] // 2
    tile, slot = tiling(piece, col)
    return operate(
        second_kernel,
        place,
        cov,
        jax.ShapeDtypeStruct((cov.shape[0], edits), F32),
        [pair],
        [pl.BlockSpec((columns, 2 * edits), lambda i, s: (0, 0))],
        pl.BlockSpec((tile, edits), slot),
        [],
        tile,
        edits,
    )


def update_kernel(basis, direct, alpha, alpha_last, resid_ref, out_ref, held):
    @pl.when(pl.program_id(0) == 0)
    def _():
        value = dot(basis[...], alpha[...]) + dot(direct[...], alpha_last[...])
        high, low = split(value)
        held[:, :128] = high
        held[:, 128:] = low

    high, low = split(resid_ref[...])
    across = ((1,), (1,))
    edits = high.shape[1]
    value = dot(held[:, :edits], high, across, None) + (
        dot(held[:, edits:], high, across, None) + dot(held[:, :edits], low, across, None)
    )
    out_ref[...] = value.astype(out_ref.dtype)


def update_step(basis, direct, alpha, alpha_last, resid):
    rows, edits = basis.shape
    features = resid.shape[0]
    tile = features // 7
    whole = pl.BlockSpec((rows, edits), lambda i: (0, 0))
    small = pl.BlockSpec((edits, edits), lambda i: (0, 0))
    return pl.pallas_call(
        update_kernel,
        out_shape=jax.ShapeDtypeStruct((rows, features), BF16),
        grid=(7,),
        in_specs=[
            whole,
            whole,
            small,
            small,
            pl.BlockSpec((tile, edits), lambda i: (i, 0)),
        ],
        out_specs=pl.BlockSpec((rows, tile), lambda i: (0, i)),
        scratch_shapes=[pltpu.VMEM((rows, 2 * edits), BF16)],
        compiler_params=pltpu.CompilerParams(dimension_semantics=("arbitrary",)),
        name="update_step",
    )(basis, direct, alpha, alpha_last, resid)


def edit(states, subject_pos, gate_weight, up_weight, down_weight, covariance, targets, *, row, col):
    edits, prompts, seq_len, _ = states.shape
    piece = down_weight.shape[2]
    hidden_units = row * col * piece
    place = jnp.stack([lax.axis_index("row"), lax.axis_index("col")]).astype(jnp.int32)
    marks = lax.broadcasted_iota(jnp.int32, (1, 1, seq_len, 1), 2) == subject_pos[:, :, None, None]
    chosen = jnp.sum(jnp.where(marks, states, jnp.zeros_like(states)), axis=2)
    token_rows = chosen.transpose(1, 0, 2).reshape(prompts * edits, -1)

    flat = [w.reshape(w.shape[0], -1) for w in (gate_weight, up_weight)]
    chunks = []
    for weight in flat:
        chunks.append(project(place, token_rows, weight, row, piece))
    gate, up = reduce_rows(chunks, row)
    hidden = jax.nn.silu(gate) * up
    keys = sum(hidden[:, p * edits : (p + 1) * edits] for p in range(prompts)) / prompts
    basis = 4.0 / math.sqrt(hidden_units) * keys
    across = ((0,), (0,))

    def cut(field):
        return [field[k * piece : (k + 1) * piece] for k in range(col)]

    def cut(field):
        return [field[k * piece : (k + 1) * piece] for k in range(col)]

    wide_basis = gather_rows(basis, row)
    terms = dot(down_weight.reshape(piece, -1), keys.astype(BF16), across, None)
    terms = with_layout_constraint(terms, Layout(major_to_minor=(0, 1)))
    terms, stacks = lax.optimization_barrier((terms, [stack for _, stack, _ in wide_basis]))
    wide_basis = [(start, stack, slots) for (start, _, slots), stack in zip(wide_basis, stacks)]
    current = lax.psum_scatter(terms, ("row", "col"), scatter_dimension=0, tiled=True)
    partial, wide_b, gram = operate_first(place, covariance, wide_basis, piece, col)
    norm_parts = fetch_all(gram, col)
    image = reduce_cols(cut(partial), col)
    norm = symmetric(sum(norm_parts, gram))
    image = image + dot(basis, norm)
    first = sum_all(dot(basis, image, across), row, col)
    wide_image = gather_rows(image, row)
    alpha, norm_inverse = solve((symmetric(first), norm), (norm, jnp.eye(edits, dtype=F32)))

    resid = basis - dot(image, alpha)
    talls = gather_cols(resid, col)
    pair_r, grams = residual_step(place, wide_b, alpha, wide_image, piece, row)
    current, pair_r = lax.optimization_barrier((current, pair_r))
    residual_t = lax.all_gather(targets - current, ("row", "col"), axis=0, tiled=True)
    gram_parts = fetch_all(grams, col)
    partial_r = operate_second(place, covariance, pair_r, piece, col)
    partial_r, grams, gram_parts, talls = lax.optimization_barrier((partial_r, grams, gram_parts, talls))
    quad = sum_all(sum(dot(tall, slot, across) for tall, slot in zip(talls, cut(partial_r))), row, col)
    grams = sum(gram_parts, grams)
    norm_next = symmetric(grams[:edits])
    mixed = grams[edits:]
    leaning = norm - dot(first, alpha)
    beta = dot(norm_inverse, norm_next)
    direction = resid + dot(basis, beta)
    rest = dot(leaning.T, leaning) + dot(beta.T, mixed) + dot(mixed.T, beta) + dot(beta.T, dot(first, beta))
    (alpha_last,) = solve((symmetric(quad + rest), norm_next))
    update = update_step(basis, direction, alpha, alpha_last, residual_t)
    return update.reshape(1, 1, piece, -1)


def solution(mesh):
    return jax.shard_map(
        functools.partial(edit, row=mesh.shape["row"], col=mesh.shape["col"]),
        mesh=mesh,
        in_specs=(
            P(None, None, None, "row"),
            P(),
            P("row", "col", None),
            P("row", "col", None),
            P("row", "col", None, None),
            P("row", "col", None),
            P(("row", "col"), None),
        ),
        out_specs=P("row", "col", None, None),
        check_vma=False,
    )
```
